32 devices in a mesh: lat: 8 (over y, x, core), grp: 4 (over z).
Axes of the slice: x: 2, y: 2, z: 4, core: 2. Of those that a mesh axis runs over, the one named last changes fastest.
Arguments:
- increments: bfloat16 [2048, 4, 16, 128], P(('lat', 'grp')), may hold values from -6 to 6
- band: int32 [2048, 1], P(('lat', 'grp')), may hold values from 0 to 7; in each aligned block of 64 rows (0 to 63, 64 to 127, ...) at most 24 rows name the same one
- tile_index: int32 [2048], P(('lat', 'grp')), may hold values from 0 to 7
- lat_offset: int32 [2048], P(('lat', 'grp')), may hold values from 0 to 12
- lon_shift: int32 [2048], P(('lat', 'grp')), may hold values from -8 to 8
- lat_frac: float32 [2048], P(('lat', 'grp')), may hold values from 0 to 1
- lon_frac: float32 [2048, 128], P(('lat', 'grp')), may hold values from 0 to 1
Outputs:
- source_adjoint: float32 [16, 4, 1024, 128], P('grp', None, 'lat')
The draws below stay inside these ranges and needn't reach their ends.
Inputs may be any that keep to these rules, and one draw needn't show every extreme that they name: In the rows of one device no band is named more than 24 times, a bound that some block reaches.
All inputs are finite; a program needn't handle non-finite values.
Results may differ from the reference program's by a relative error of at most 0.0045.
Values may be sent and summed in bfloat16 or wider, within the bound.
A program may use at most 64 MiB of HBM per device.

```python
import math
import jax
import jax.numpy as jnp
import numpy as np
from jax import lax

F = 4
L = 16
POINTS = 128
TL = 16
TILES_DEV = 8
ROWS_DEV = 64
CAP = 24
ROWS = 2048
TILE_ROWS = 1024
N_LAT = 8


def place_ends(array, stream_key, low, top_value):
    dims = array.shape
    spot = [jax.random.randint(jax.random.fold_in(stream_key, axis), (), 0, dims[axis]) for axis in range(len(dims))]
    array = array.at[tuple(spot)].set(low)
    longest = dims.index(max(dims))
    spot[longest] = (spot[longest] + 1) % dims[longest]
    return array.at[tuple(spot)].set(top_value)


def level_of(rng, dims, split, low, high):
    level, own = 1.0, jax.random.fold_in(rng, 6)
    for axis_at, blocks in split:
        draws = jnp.exp(jax.random.uniform(jax.random.fold_in(own, axis_at), (blocks,), jnp.float32, low / len(split), high / len(split)))
        level = level * jnp.repeat(draws, dims[axis_at] // blocks).reshape([-1 if axis == axis_at else 1 for axis in range(len(dims))])
    return level


def deal_out(key, own, number, rows, amount, top, reach, skew):
    order = jax.random.permutation(key, amount)
    heavy_load, common = shares(amount, rows * top, reach, skew, True), shares(amount, rows * top, reach, skew, False)
    places = jnp.arange(amount)

    def named(lengths, rotation):
        used = int((lengths > 0).sum())
        fixed = max(1, used // 4)
        shifted = fixed + (places - fixed + rotation * (used - fixed)) % max(1, amount - fixed)
        return jnp.zeros((amount,), jnp.int32).at[order[jnp.where(places < fixed, places, shifted)]].set(jnp.asarray(lengths, jnp.int32))

    lengths = jnp.where(number % 4 == 0, named(heavy_load, number // 4), named(common, number - number // 4 - 1))
    mixed = jax.random.permutation(jax.random.fold_in(own, 3), amount)
    giver, taker = mixed[0:amount // 2 * 2:2], mixed[1:amount // 2 * 2:2]
    room = jnp.minimum(lengths[giver] - 1, reach - lengths[taker]) // 2
    room = jnp.where((giver == order[0]) | (taker == order[0]) | (lengths[taker] == 0), 0, jnp.maximum(room, 0))
    shifted = jax.random.randint(jax.random.fold_in(own, 4), (amount // 2,), 0, 1 << 20) % (room + 1)
    lengths = lengths.at[giver].add(-shifted).at[taker].add(shifted)
    members = jnp.searchsorted(jnp.cumsum(lengths), jnp.arange(rows * top), side="right").astype(jnp.int32)
    grid = members.reshape(top, rows).T
    grid = grid[jax.random.permutation(jax.random.fold_in(own, 1), rows)]
    rotation = jax.random.randint(jax.random.fold_in(own, 2), (rows, 1), 0, top)
    return jnp.take_along_axis(grid, (jnp.arange(top)[None, :] + rotation) % top, axis=1)


def shares(amount, total, limit, skew, full):
    portions = [(1 << 20) // math.isqrt(grade ** skew) + 1 for grade in range(1, amount + 1)]
    largest = limit if full else min(limit, max(-(-total // amount), total * portions[0] // sum(portions)))
    least = 1 if total - largest >= amount - 1 else 0
    counts, rest = [largest] + [least] * (amount - 1), total - largest - least * (amount - 1)
    while rest > 0:
        movable = [i for i in range(1, amount) if counts[i] < largest] or [i for i in range(1, amount) if counts[i] < limit]
        whole, left = sum([portions[i] for i in movable]), rest
        for i in movable:
            more = min(limit - counts[i], max(1, left * portions[i] // whole), rest)
            counts[i] = counts[i] + more
            rest = rest - more
    return np.array(counts)


def noise(own_key, dims, deviation, limit, pieces=(), held_as=jnp.bfloat16):
    result = deviation * jax.random.normal(own_key, dims, jnp.float32)
    if pieces:
        result = result * level_of(own_key, dims, pieces, -0.22, 0.18)
    return jnp.clip(result, -limit, limit).astype(held_as)


def setup_inputs(seed: int = 0) -> dict:
    arg_keys = jax.random.split(jax.random.key(seed), 8)
    increments = noise(arg_keys[0], (ROWS, F, L, POINTS), 1.0, 6.0, ((0, 32),))
    band_keys = jax.random.split(jax.random.fold_in(arg_keys[1], 1), ROWS // ROWS_DEV)
    band_turns = jax.random.permutation(jax.random.fold_in(arg_keys[1], 3), ROWS // ROWS_DEV)
    band = jax.vmap(lambda own, number: deal_out(jax.random.fold_in(arg_keys[1], 2), own, number, ROWS_DEV, N_LAT, 1, CAP, 2))(band_keys, band_turns).reshape((ROWS, 1))
    tile_index = place_ends(jax.random.randint(arg_keys[2], (ROWS,), 0, TILES_DEV), jax.random.fold_in(arg_keys[2], 1), 0, TILES_DEV - 1).astype(jnp.int32)
    lat_offset = place_ends(jax.random.randint(arg_keys[3], (ROWS,), 0, TL - 3), jax.random.fold_in(arg_keys[3], 1), 0, (TL - 3) - 1).astype(jnp.int32)
    lon_shift = place_ends(jax.random.randint(arg_keys[4], (ROWS,), -8, 9), jax.random.fold_in(arg_keys[4], 1), -8, 8).astype(jnp.int32)
    lat_frac = jnp.clip(1.0 * jax.random.uniform(arg_keys[5], (ROWS,), jnp.float32) ** level_of(arg_keys[5], (ROWS,), ((0, 32),), -0.2, 0.2), 0.0, 1.0)
    lon_frac = jnp.clip(1.0 * jax.random.uniform(arg_keys[6], (ROWS, POINTS), jnp.float32) ** level_of(arg_keys[6], (ROWS, POINTS), ((0, 32),), -0.2, 0.2), 0.0, 1.0)
    return dict(increments=increments, band=band, tile_index=tile_index, lat_offset=lat_offset, lon_shift=lon_shift, lat_frac=lat_frac, lon_frac=lon_frac)


def lagrange(fraction):
    return [-fraction * (fraction - 1.0) * (fraction - 2.0) / 6.0,
            (fraction + 1.0) * (fraction - 1.0) * (fraction - 2.0) / 2.0,
            -(fraction + 1.0) * fraction * (fraction - 2.0) / 2.0,
            (fraction + 1.0) * fraction * (fraction - 1.0) / 6.0]


def reference(increments, band, tile_index, lat_offset, lon_shift, lat_frac, lon_frac):
    row_count = increments.shape[0]
    width = math.gcd(row_count, 512)
    lon_weight = [w.astype(jnp.bfloat16) for w in lagrange(lon_frac)]
    lat_weight = [w.astype(jnp.bfloat16) for w in lagrange(lat_frac)]
    band_base = band[:, 0] * (TILES_DEV * TL) + lat_offset
    here_rows = (band_base + tile_index * TL).astype(jnp.int32)
    next_rows = (band_base + ((tile_index + 1) % TILES_DEV) * TL).astype(jnp.int32)
    prev_rows = (band_base + ((tile_index + TILES_DEV - 1) % TILES_DEV) * TL).astype(jnp.int32)
    columns = jnp.arange(POINTS, dtype=jnp.int32)
    low_half = (columns < POINTS // 2)[None, None, None, :]

    def one_block(total, number):
        first = (number * width).astype(jnp.int32)
        values = lax.dynamic_slice_in_dim(increments, first, width, 0).astype(jnp.float32)
        shifts = lax.dynamic_slice_in_dim(lon_shift, first, width, 0)
        own = jnp.zeros(values.shape, jnp.float32)
        spill = jnp.zeros(values.shape, jnp.float32)
        for m in range(4):
            weight = lax.dynamic_slice_in_dim(lon_weight[m], first, width, 0).astype(jnp.float32)
            scaled = values * weight[:, None, None, :]
            raw = (columns[None, :] - shifts[:, None] - m + 1).astype(jnp.int32)
            inside = (raw >= 0) & (raw < POINTS)
            source = (raw % POINTS).astype(jnp.int32)
            source = jnp.broadcast_to(source[:, None, None, :], scaled.shape)
            picked = jnp.take_along_axis(scaled, source, axis=3)
            inside = inside[:, None, None, :]
            own = own + jnp.where(inside, picked, 0.0)
            spill = spill + jnp.where(inside, 0.0, picked)
        own = lax.optimization_barrier(own.astype(jnp.bfloat16)).astype(jnp.float32)
        spill = lax.optimization_barrier(spill.astype(jnp.bfloat16)).astype(jnp.float32)
        spill_next = jnp.where(low_half, spill, 0.0)
        spill_prev = jnp.where(low_half, 0.0, spill)
        rows_here = lax.dynamic_slice_in_dim(here_rows, first, width, 0)
        rows_next = lax.dynamic_slice_in_dim(next_rows, first, width, 0)
        rows_prev = lax.dynamic_slice_in_dim(prev_rows, first, width, 0)
        for k in range(4):
            weight = lax.dynamic_slice_in_dim(lat_weight[k], first, width, 0).astype(jnp.float32)[:, None, None, None]
            total = total.at[rows_here + k].add(weight * own)
            total = total.at[rows_next + k].add(weight * spill_next)
            total = total.at[rows_prev + k].add(weight * spill_prev)
        return total, None

    total = jnp.zeros((TILE_ROWS, F, L, POINTS), jnp.float32)
    total, _ = lax.scan(one_block, total, jnp.arange(row_count // width, dtype=jnp.int32))
    return jnp.transpose(total, (2, 1, 0, 3))
```

```python
import functools
import math

import jax
import jax.numpy as jnp
from jax import lax
from jax.experimental import pallas as pl
from jax.experimental.pallas import tpu as pltpu
from jax.sharding import PartitionSpec as P

TL = 16
TILES_DEV = 8


def lagrange(fraction):
    return [
        -fraction * (fraction - 1.0) * (fraction - 2.0) / 6.0,
        (fraction + 1.0) * (fraction - 1.0) * (fraction - 2.0) / 2.0,
        -(fraction + 1.0) * fraction * (fraction - 2.0) / 2.0,
        (fraction + 1.0) * fraction * (fraction - 1.0) / 6.0,
    ]


def lon_adjoint(increments, lon_shift, lon_frac):
    row_count, fields, levels, points = increments.shape
    lon_weight = [w.astype(jnp.bfloat16) for w in lagrange(lon_frac)]
    source = jnp.arange(points, dtype=jnp.int32)[None, :, None]
    target = jnp.arange(points, dtype=jnp.int32)[None, None, :]
    width = math.gcd(row_count, 32)
    nothing = jnp.zeros((), jnp.bfloat16)

    def one_block(number):
        first = number * width
        shifts = lax.dynamic_slice_in_dim(lon_shift, first, width, 0)
        own_matrix = jnp.zeros((width, points, points), jnp.bfloat16)
        spill_matrix = jnp.zeros((width, points, points), jnp.bfloat16)
        for m in range(4):
            weight = lax.dynamic_slice_in_dim(lon_weight[m], first, width, 0)[:, :, None]
            landing = source + shifts[:, None, None] + m - 1
            own_matrix = own_matrix + jnp.where(target == landing, weight, nothing)
            wrapped = (target == landing - points) | (target == landing + points)
            spill_matrix = spill_matrix + jnp.where(wrapped, weight, nothing)
        values = lax.dynamic_slice_in_dim(increments, first, width, 0)
        own = jnp.einsum(
            "bflj,bjc->bflc", values, own_matrix, preferred_element_type=jnp.float32
        ).astype(jnp.bfloat16)
        spill = jnp.einsum(
            "bflj,bjc->bflc", values, spill_matrix, preferred_element_type=jnp.float32
        ).astype(jnp.bfloat16)
        return (own, spill)

    own, spill = lax.map(one_block, jnp.arange(row_count // width, dtype=jnp.int32))
    return (
        own.reshape(row_count, fields, levels, points),
        spill.reshape(row_count, fields, levels, points),
    )


def tile_terms(columns, own_rows, spill_rows):
    points = own_rows.shape[3]
    low_half = (jnp.arange(points, dtype=jnp.int32) < points // 2)[None, None, None, :]
    nothing = jnp.zeros((), jnp.bfloat16)
    spill_next = jnp.where(low_half, spill_rows, nothing)
    spill_prev = jnp.where(low_half, nothing, spill_rows)
    result = jnp.einsum("sq,sflc->lfqc", columns[0], own_rows, preferred_element_type=jnp.float32)
    result = result + jnp.einsum(
        "sq,sflc->lfqc", columns[1], spill_next, preferred_element_type=jnp.float32
    )
    return result + jnp.einsum(
        "sq,sflc->lfqc", columns[2], spill_prev, preferred_element_type=jnp.float32
    )


def by_slots(increments, band, tile_index, lat_offset, lon_shift, lat_frac, lon_frac):
    row_count, fields, levels, points = increments.shape
    n_lat = lax.axis_size("lat")
    capacity = 3 * row_count // n_lat
    tile_rows = TILES_DEV * TL
    own, spill = lon_adjoint(increments, lon_shift, lon_frac)
    lat_weight = [w.astype(jnp.bfloat16) for w in lagrange(lat_frac)]
    tile_slots = jnp.arange(tile_rows, dtype=jnp.int32)[None, :]
    nothing = jnp.zeros((), jnp.bfloat16)

    def stencil_columns(tile_number):
        base_row = tile_number * TL + lat_offset
        table = jnp.zeros((row_count, tile_rows), jnp.bfloat16)
        for k in range(4):
            table = table + jnp.where(
                tile_slots == base_row[:, None] + k, lat_weight[k][:, None], nothing
            )
        return table

    here_columns = stencil_columns(tile_index)
    next_columns = stencil_columns((tile_index + 1) % TILES_DEV)
    prev_columns = stencil_columns((tile_index + TILES_DEV - 1) % TILES_DEV)
    destination = band[:, 0]
    one_hot = (destination[:, None] == jnp.arange(n_lat, dtype=jnp.int32)[None, :]).astype(
        jnp.int32
    )
    position = jnp.sum(jnp.cumsum(one_hot, axis=0) * one_hot, axis=1) - 1
    slot_index = destination * capacity + position

    def to_slots(values):
        empty = jnp.zeros((n_lat * capacity,) + values.shape[1:], jnp.bfloat16)
        placed = empty.at[slot_index].set(values)
        return placed.reshape((n_lat, capacity) + values.shape[1:])

    send_own = to_slots(own)
    send_spill = to_slots(spill)
    send_here = to_slots(here_columns)
    send_next = to_slots(next_columns)
    send_prev = to_slots(prev_columns)
    got = (
        lax.all_to_all(send_own, "lat", split_axis=0, concat_axis=0, tiled=True),
        lax.all_to_all(send_spill, "lat", split_axis=0, concat_axis=0, tiled=True),
        lax.all_to_all(send_here, "lat", split_axis=0, concat_axis=0, tiled=True),
        lax.all_to_all(send_next, "lat", split_axis=0, concat_axis=0, tiled=True),
        lax.all_to_all(send_prev, "lat", split_axis=0, concat_axis=0, tiled=True),
    )
    flat_own = got[0].reshape(-1, fields, levels, points)
    flat_spill = got[1].reshape(-1, fields, levels, points)
    flat_columns = (
        got[2].reshape(-1, tile_rows),
        got[3].reshape(-1, tile_rows),
        got[4].reshape(-1, tile_rows),
    )
    return lax.psum_scatter(
        tile_terms(flat_columns, flat_own, flat_spill), "grp", scatter_dimension=0, tiled=True
    )


MESH = pl.DeviceIdType.MESH


def fused_kernel(n_lat, n_grp, x_ref, frac_ref, band_ref, tile_ref, first_ref, shift_ref, part_ref, out_ref,
                 meta_ref, fs, xs, fr, wl, am, rb, pb, s1, r1, q1, s2, q2, s3, r3,
                 z_send, z_recv, f_send, f_recv, n_send, n_recv, x_send, x_recv,
                 d_send, d_recv, p_send, p_recv, e_send, e_recv, o_send, o_recv, loc_sem):
    lat = lax.axis_index("lat")
    grp = lax.axis_index("grp")
    chip, core = lat // 2, lat % 2
    other = 1 - core
    mate = chip * 2 + other
    n_chip = n_lat // 2
    units, rows, points = xs.shape[1:]
    tile_rows = TILES_DEV * TL

    def toggled(bit):
        return chip + bit * (1 - 2 * ((chip // bit) % 2))

    across = (toggled(1), toggled(2))
    opposite = toggled(1) + toggled(2) - chip
    parity = (core, other)
    first = tuple(across[0] * (1 - q) + across[1] * q for q in parity)
    second = tuple(across[1] * (1 - q) + across[0] * q for q in parity)

    def source(d):
        bits = [1 << n for n in range(n_grp.bit_length()) if d & (1 << n)]
        return grp + sum(bit * (1 - 2 * ((grp // bit) % 2)) for bit in bits)

    barrier = pltpu.get_barrier_semaphore()
    for d in range(1, n_grp):
        for q in parity:
            pl.semaphore_signal(barrier, inc=1, device_id=(chip * 2 + q, source(d)), device_id_type=MESH)
    pl.semaphore_signal(barrier, inc=1, device_id=(mate, grp), device_id_type=MESH)
    for to in across:
        for q in parity:
            pl.semaphore_signal(barrier, inc=1, device_id=(to * 2 + q, grp), device_id_type=MESH)

    def coded(fraction):
        return jnp.round(fraction * 65535.0) - 32768.0

    def decoded(code):
        return (code.astype(jnp.float32) + 32768.0) * (1.0 / 65535.0)

    meta_ref[...] = jnp.zeros_like(meta_ref)
    meta_ref[0:1, 0:rows] = band_ref[...].astype(jnp.float32)
    meta_ref[1:2, 0:rows] = (tile_ref[...] * TL + first_ref[...]).astype(jnp.float32)
    meta_ref[2:3, 0:rows] = shift_ref[...].astype(jnp.float32)
    meta_ref[3:4, 0:rows] = coded(part_ref[...])
    fs[0:rows] = coded(frac_ref[...]).astype(jnp.int32).astype(jnp.int16)
    fs[rows:rows + 8] = meta_ref[...].astype(jnp.int32).astype(jnp.int16)

    pl.semaphore_wait(barrier, 2 * (n_grp - 1) + 1 + 4)

    def remote(src, dst, send, recv, to):
        return pltpu.make_async_remote_copy(
            src_ref=src, dst_ref=dst, send_sem=send, recv_sem=recv, device_id=to, device_id_type=MESH
        )

    def f_copy(d, g):
        return remote(fs, fr.at[g], f_send.at[d], f_recv.at[g], (lat, source(d)))

    def n_copy(d):
        g = source(d)
        src = fs if d == 0 else fr.at[g]
        return remote(src, fr.at[n_grp + g], n_send.at[d], n_recv.at[g], (mate, grp))

    def z_copy(d, v, j, g):
        to, q = source(d), parity[j]
        return remote(x_ref.at[(to * 2 + q) * units + v], xs.at[j * n_grp + g, v],
                      z_send.at[d, j, v], z_recv.at[g, j, v], (chip * 2 + q, to))

    def x_copy():
        return remote(x_ref.at[pl.ds((grp * 2 + other) * units, units)], xs.at[n_grp + grp],
                      x_send, x_recv, (mate, grp))

    def d_copy(v, j):
        return remote(s1.at[v, j, 0], q1.at[v, j], d_send.at[v, j], d_recv.at[v, j], (first[j] * 2 + parity[j], grp))

    def p_copy(v, j):
        return remote(s1.at[v, j, 1], r1.at[v, j], p_send.at[v, j], p_recv.at[v, j], (first[j] * 2 + core, grp))

    def e_copy(v, j):
        return remote(s2.at[v, j], q2.at[v, j], e_send.at[v, j], e_recv.at[v, j], (second[j] * 2 + parity[j], grp))

    def o_copy(v):
        return remote(s3.at[v], r3.at[v], o_send.at[v], o_recv.at[v], (mate, grp))

    own_x = pltpu.make_async_copy(x_ref.at[pl.ds((grp * 2 + core) * units, units)], xs.at[grp], loc_sem)
    for d in range(1, n_grp):
        f_copy(n_grp - d, grp).start()
    n_copy(0).start()
    for v in range(units):
        for near in range(2 * v, min(2 * v + 2, units)):
            for j in range(2):
                z_copy(1, near, j, grp).start()
        for d in range(2, n_grp):
            for j in range(2):
                z_copy(d, v, j, grp).start()
    own_x.start()
    x_copy().start()

    lane = lax.broadcasted_iota(jnp.int32, (rows, points), 1)
    eye = lax.broadcasted_iota(jnp.int32, (rows, points), 0) == lane
    steps = (1, 2, 4, 8, 16)

    def turn(values, amount):
        return pltpu.roll(values, amount % points, 1)

    def weights_of(at, code):
        shift_lanes = code[rows:rows + 8].astype(jnp.int32)[2:3].astype(jnp.float32)
        diagonal = jnp.where(eye, shift_lanes, 0.0).astype(jnp.bfloat16)
        shift = jnp.dot(
            diagonal, jnp.ones((points, points), jnp.bfloat16), preferred_element_type=jnp.float32
        ).astype(jnp.int32)
        bits = shift + 8
        for m, weight in enumerate(lagrange(decoded(code[0:rows].astype(jnp.int32)))):
            weight = weight.astype(jnp.bfloat16).astype(jnp.float32)
            for step in steps:
                weight = jnp.where((bits & step) != 0, turn(weight, step), weight)
            weight = turn(weight, m - 9)
            raw = lane - shift - (m - 1)
            inside = (raw >= 0) & (raw < points)
            wl[at, m] = jnp.where(inside, weight, 0.0)
            wl[at, 4 + m] = jnp.where(inside, 0.0, weight)
        wl[at, 8] = bits.astype(jnp.float32)

    wide = lax.broadcasted_iota(jnp.int32, (8, 2 * rows), 1)
    slot = lax.broadcasted_iota(jnp.int32, (tile_rows, 2 * rows), 0)

    def meta_of(at):
        return fr[at, rows:rows + 8].astype(jnp.int32).astype(jnp.float32)

    def table_of(at):
        both = jnp.where(wide < rows, meta_of(at), pltpu.roll(meta_of(at + 1), rows, 1))
        band = both[0:1].astype(jnp.int32)
        place = both[1:2].astype(jnp.int32)
        lat_weight = [w.astype(jnp.bfloat16).astype(jnp.float32) for w in lagrange(decoded(both[3:4]))]
        for j in range(2):
            for e, to in enumerate((chip, first[j], second[j], opposite)):
                far = slot - jnp.where(band == to * 2 + parity[j], place, -(1 << 20))
                table = jnp.zeros(far.shape, jnp.float32)
                for k in range(4):
                    table = jnp.where(far == k, lat_weight[k], table)
                am[pl.ds((j * n_chip + e) * tile_rows, tile_rows), pl.ds(at * rows, 2 * rows)] = table.astype(jnp.bfloat16)

    fr[grp] = fs[...]
    weights_of(grp, fs[...])
    for d in range(1, n_grp):
        f_copy(d, source(d)).wait_recv()
        n_copy(d).start()
        weights_of(source(d), fr[source(d)])
    for g in range(0, n_grp, 2):
        table_of(g)
    for d in range(n_grp):
        g = source(d)
        n_copy(d).wait_recv()
        weights_of(n_grp + g, fr[n_grp + g])
    for g in range(0, n_grp, 2):
        table_of(n_grp + g)
    own_x.wait()
    x_copy().wait_recv()

    def lon(at, v):
        bits = wl[at, 8].astype(jnp.int32)
        moved = xs[at, v].astype(jnp.float32)
        for step in steps:
            moved = jnp.where((bits & step) != 0, turn(moved, step), moved)
        own, spill = 0.0, 0.0
        for m in range(4):
            x = turn(moved, m - 9)
            own = own + x * wl[at, m]
            spill = spill + x * wl[at, 4 + m]
        place = pl.ds(at * rows, rows)
        rb[v % 2, place, 0:points] = own.astype(jnp.bfloat16)
        rb[v % 2, place, points:2 * points] = spill.astype(jnp.bfloat16)

    low = lax.broadcasted_iota(jnp.int32, (tile_rows, points), 1) < points // 2

    def arrive(v):
        for d in range(n_grp):
            for j in range(2):
                if d:
                    z_copy(d, v, j, source(d)).wait_recv()
            for j in range(2):
                lon(j * n_grp + source(d), v)

    def depart(v):
        whole = jnp.dot(am[...], rb[v % 2], preferred_element_type=jnp.float32)
        for j in range(2):
            for e in (3, 1, 2, 0):
                at = (j * n_chip + e) * tile_rows
                both = whole[at:at + tile_rows]
                own, spill = both[:, :points], both[:, points:]
                ahead = jnp.concatenate([spill[-TL:], spill[:-TL]], axis=0)
                behind = jnp.concatenate([spill[TL:], spill[:TL]], axis=0)
                total = own + jnp.where(low, ahead, behind)
                if e == 3:
                    s1[v, j, 1] = total.astype(jnp.bfloat16)
                    p_copy(v, j).start()
                elif e == 1:
                    s1[v, j, 0] = total.astype(jnp.bfloat16)
                    d_copy(v, j).start()
                elif e == 2:
                    pb[v % 2, j] = total
                elif j == 0:
                    out_ref[core * units + v] = total
                else:
                    s3[v] = total
                    o_copy(v).start()

    def middle(v):
        for j in range(2):
            p_copy(v, j).wait_recv()
            s2[v, j] = (pb[v % 2, j] + r1[v, j].astype(jnp.float32)).astype(jnp.bfloat16)
            e_copy(v, j).start()

    def finish(v):
        for j in range(2):
            d_copy(v, j).wait_recv()
            e_copy(v, j).wait_recv()
            at = parity[j] * units + v
            if j:
                o_copy(v).wait_recv()
            mine = r3[v] if j else out_ref[at]
            out_ref[at] = mine + q1[v, j].astype(jnp.float32) + q2[v, j].astype(jnp.float32)

    def chunk(v, carry):
        @pl.when(v < units)
        def _():
            arrive(v)
            depart(v)

        @pl.when((v >= 1) & (v < units + 1))
        def _():
            middle(v - 1)

        @pl.when(v >= 2)
        def _():
            finish(v - 2)

        return carry

    lax.fori_loop(0, units + 2, chunk, 0)

    n_copy(0).wait_send()
    x_copy().wait_send()
    for d in range(1, n_grp):
        f_copy(d, grp).wait_send()
        n_copy(d).wait_send()
    for v in range(units):
        o_copy(v).wait_send()
        for j in range(2):
            for d in range(1, n_grp):
                z_copy(d, v, j, grp).wait_send()
            d_copy(v, j).wait_send()
            p_copy(v, j).wait_send()
            e_copy(v, j).wait_send()


def fused(increments, band, tile_index, lat_offset, lon_shift, lat_frac, lon_frac):
    rows, fields, all_levels, points = increments.shape
    n_lat, n_grp = lax.axis_size("lat"), lax.axis_size("grp")
    n_chip = n_lat // 2
    levels = all_levels // n_grp
    tile_rows = TILES_DEV * TL
    units = levels * fields // 2
    x = jnp.transpose(increments, (2, 1, 0, 3)).reshape(all_levels * fields, rows, points)
    small = [a.reshape(1, rows) for a in (band, tile_index, lat_offset, lon_shift, lat_frac)]
    bf16, f32 = jnp.bfloat16, jnp.float32
    dma = pltpu.SemaphoreType.DMA
    sums = (units, 2, tile_rows, points)
    return pl.pallas_call(
        functools.partial(fused_kernel, n_lat, n_grp),
        out_shape=jax.ShapeDtypeStruct((2 * units, tile_rows, points), f32),
        in_specs=[pl.BlockSpec(memory_space=pltpu.VMEM)] * 7,
        out_specs=pl.BlockSpec(memory_space=pltpu.VMEM),
        scratch_shapes=[
            pltpu.VMEM((8, points), f32),
            pltpu.VMEM((rows + 8, points), jnp.int16),
            pltpu.VMEM((2 * n_grp, units, rows, points), bf16),
            pltpu.VMEM((2 * n_grp, rows + 8, points), jnp.int16),
            pltpu.VMEM((2 * n_grp, 9, rows, points), f32),
            pltpu.VMEM((n_lat * tile_rows, n_grp * 2 * rows), bf16),
            pltpu.VMEM((2, n_grp * 2 * rows, 2 * points), bf16),
            pltpu.VMEM((2, 2, tile_rows, points), f32),
            pltpu.VMEM((units, 2, 2, tile_rows, points), bf16),
            pltpu.VMEM(sums, bf16),
            pltpu.VMEM(sums, bf16),
            pltpu.VMEM(sums, bf16),
            pltpu.VMEM(sums, bf16),
            pltpu.VMEM((units, tile_rows, points), f32),
            pltpu.VMEM((units, tile_rows, points), f32),
            dma((n_grp, 2, units)),
            dma((n_grp, 2, units)),
            dma((n_grp,)),
            dma((n_grp,)),
            dma((n_grp,)),
            dma((n_grp,)),
            dma,
            dma,
            dma((units, 2)),
            dma((units, 2)),
            dma((units, 2)),
            dma((units, 2)),
            dma((units, 2)),
            dma((units, 2)),
            dma((units,)),
            dma((units,)),
            dma,
        ],
        compiler_params=pltpu.CompilerParams(
            collective_id=0, has_side_effects=True, vmem_limit_bytes=40 * 1024 * 1024
        ),
    )(x, lon_frac, *small).reshape(levels, fields, tile_rows, points)


def solution(mesh):
    in_specs = (
        P(("lat", "grp"), None, None, None),
        P(("lat", "grp"), None),
        P(("lat", "grp")),
        P(("lat", "grp")),
        P(("lat", "grp")),
        P(("lat", "grp")),
        P(("lat", "grp"), None),
    )
    out_specs = P("grp", None, "lat", None)
    n_lat, n_grp = mesh.shape["lat"], mesh.shape["grp"]

    def local(increments, *rest):
        rows = increments.shape[0]
        dense_rows = n_lat // 2 * TILES_DEV * TL
        slot_rows = n_grp * n_lat * (3 * rows // n_lat)
        grid = n_lat == 8 and n_grp > 1 and n_grp & (n_grp - 1) == 0
        step = fused if grid and dense_rows <= slot_rows else by_slots
        return step(increments, *rest)

    return jax.shard_map(local, mesh=mesh, in_specs=in_specs, out_specs=out_specs, check_vma=False)
```

```python
import functools
import math

import jax
import jax.numpy as jnp
from jax import lax
from jax.experimental import pallas as pl
from jax.experimental.pallas import tpu as pltpu
from jax.sharding import PartitionSpec as P

TL = 16
TILES_DEV = 8


def lagrange(fraction):
    return [
        -fraction * (fraction - 1.0) * (fraction - 2.0) / 6.0,
        (fraction + 1.0) * (fraction - 1.0) * (fraction - 2.0) / 2.0,
        -(fraction + 1.0) * fraction * (fraction - 2.0) / 2.0,
        (fraction + 1.0) * fraction * (fraction - 1.0) / 6.0,
    ]


def lon_adjoint(increments, lon_shift, lon_frac):
    row_count, fields, levels, points = increments.shape
    lon_weight = [w.astype(jnp.bfloat16) for w in lagrange(lon_frac)]
    source = jnp.arange(points, dtype=jnp.int32)[None, :, None]
    target = jnp.arange(points, dtype=jnp.int32)[None, None, :]
    width = math.gcd(row_count, 32)
    nothing = jnp.zeros((), jnp.bfloat16)

    def one_block(number):
        first = number * width
        shifts = lax.dynamic_slice_in_dim(lon_shift, first, width, 0)
        own_matrix = jnp.zeros((width, points, points), jnp.bfloat16)
        spill_matrix = jnp.zeros((width, points, points), jnp.bfloat16)
        for m in range(4):
            weight = lax.dynamic_slice_in_dim(lon_weight[m], first, width, 0)[:, :, None]
            landing = source + shifts[:, None, None] + m - 1
            own_matrix = own_matrix + jnp.where(target == landing, weight, nothing)
            wrapped = (target == landing - points) | (target == landing + points)
            spill_matrix = spill_matrix + jnp.where(wrapped, weight, nothing)
        values = lax.dynamic_slice_in_dim(increments, first, width, 0)
        own = jnp.einsum(
            "bflj,bjc->bflc", values, own_matrix, preferred_element_type=jnp.float32
        ).astype(jnp.bfloat16)
        spill = jnp.einsum(
            "bflj,bjc->bflc", values, spill_matrix, preferred_element_type=jnp.float32
        ).astype(jnp.bfloat16)
        return (own, spill)

    own, spill = lax.map(one_block, jnp.arange(row_count // width, dtype=jnp.int32))
    return (
        own.reshape(row_count, fields, levels, points),
        spill.reshape(row_count, fields, levels, points),
    )


def tile_terms(columns, own_rows, spill_rows):
    points = own_rows.shape[3]
    low_half = (jnp.arange(points, dtype=jnp.int32) < points // 2)[None, None, None, :]
    nothing = jnp.zeros((), jnp.bfloat16)
    spill_next = jnp.where(low_half, spill_rows, nothing)
    spill_prev = jnp.where(low_half, nothing, spill_rows)
    result = jnp.einsum("sq,sflc->lfqc", columns[0], own_rows, preferred_element_type=jnp.float32)
    result = result + jnp.einsum(
        "sq,sflc->lfqc", columns[1], spill_next, preferred_element_type=jnp.float32
    )
    return result + jnp.einsum(
        "sq,sflc->lfqc", columns[2], spill_prev, preferred_element_type=jnp.float32
    )


def by_slots(increments, band, tile_index, lat_offset, lon_shift, lat_frac, lon_frac):
    row_count, fields, levels, points = increments.shape
    n_lat = lax.axis_size("lat")
    capacity = 3 * row_count // n_lat
    tile_rows = TILES_DEV * TL
    own, spill = lon_adjoint(increments, lon_shift, lon_frac)
    lat_weight = [w.astype(jnp.bfloat16) for w in lagrange(lat_frac)]
    tile_slots = jnp.arange(tile_rows, dtype=jnp.int32)[None, :]
    nothing = jnp.zeros((), jnp.bfloat16)

    def stencil_columns(tile_number):
        base_row = tile_number * TL + lat_offset
        table = jnp.zeros((row_count, tile_rows), jnp.bfloat16)
        for k in range(4):
            table = table + jnp.where(
                tile_slots == base_row[:, None] + k, lat_weight[k][:, None], nothing
            )
        return table

    here_columns = stencil_columns(tile_index)
    next_columns = stencil_columns((tile_index + 1) % TILES_DEV)
    prev_columns = stencil_columns((tile_index + TILES_DEV - 1) % TILES_DEV)
    destination = band[:, 0]
    one_hot = (destination[:, None] == jnp.arange(n_lat, dtype=jnp.int32)[None, :]).astype(
        jnp.int32
    )
    position = jnp.sum(jnp.cumsum(one_hot, axis=0) * one_hot, axis=1) - 1
    slot_index = destination * capacity + position

    def to_slots(values):
        empty = jnp.zeros((n_lat * capacity,) + values.shape[1:], jnp.bfloat16)
        placed = empty.at[slot_index].set(values)
        return placed.reshape((n_lat, capacity) + values.shape[1:])

    send_own = to_slots(own)
    send_spill = to_slots(spill)
    send_here = to_slots(here_columns)
    send_next = to_slots(next_columns)
    send_prev = to_slots(prev_columns)
    got = (
        lax.all_to_all(send_own, "lat", split_axis=0, concat_axis=0, tiled=True),
        lax.all_to_all(send_spill, "lat", split_axis=0, concat_axis=0, tiled=True),
        lax.all_to_all(send_here, "lat", split_axis=0, concat_axis=0, tiled=True),
        lax.all_to_all(send_next, "lat", split_axis=0, concat_axis=0, tiled=True),
        lax.all_to_all(send_prev, "lat", split_axis=0, concat_axis=0, tiled=True),
    )
    flat_own = got[0].reshape(-1, fields, levels, points)
    flat_spill = got[1].reshape(-1, fields, levels, points)
    flat_columns = (
        got[2].reshape(-1, tile_rows),
        got[3].reshape(-1, tile_rows),
        got[4].reshape(-1, tile_rows),
    )
    return lax.psum_scatter(
        tile_terms(flat_columns, flat_own, flat_spill), "grp", scatter_dimension=0, tiled=True
    )


MESH = pl.DeviceIdType.MESH
BLOCKS = ((0, 3), (1, 3), (0, 1), (1, 1), (1, 0), (0, 2), (1, 2), (0, 0))
WINDOW = 2


def fused_kernel(n_lat, n_grp, fields, x_hbm, frac_hbm, band_hbm, tile_hbm, first_hbm, shift_hbm, part_hbm, out_ref,
                 frac_ref, band_ref, tile_ref, first_ref, shift_ref, part_ref, xn, xf, x_ref, meta_ref, fs, xs, fr, wl, am, rb, pb, s1, r1, q1, s2, q2, s3, r3,
                 z_send, z_recv, f_send, f_recv, n_send, n_recv, x_send, x_recv,
                 d_send, d_recv, p_send, p_recv, e_send, e_recv, o_send, o_recv, loc_sem, in_sem, small_sem):
    lat = lax.axis_index("lat")
    grp = lax.axis_index("grp")
    chip, core = lat // 2, lat % 2
    other = 1 - core
    mate = chip * 2 + other
    n_chip = n_lat // 2
    units, rows, points = xs.shape[1:]
    tile_rows = TILES_DEV * TL

    def toggled(bit):
        return chip + bit * (1 - 2 * ((chip // bit) % 2))

    across = (toggled(1), toggled(2))
    opposite = toggled(1) + toggled(2) - chip
    parity = (core, other)
    small = [pltpu.make_async_copy(src, dst, small_sem.at[n]) for n, (src, dst) in enumerate(
        ((frac_hbm, frac_ref), (band_hbm, band_ref), (tile_hbm, tile_ref), (first_hbm, first_ref),
         (shift_hbm, shift_ref), (part_hbm, part_ref)))]
    for copy in small:
        copy.start()
    pieces = in_sem.shape[0]
    stretch = xn.shape[0] // pieces
    loads = [pltpu.make_async_copy(x_hbm.at[pl.ds(n * stretch, stretch)], xn.at[pl.ds(n * stretch, stretch)], in_sem.at[n])
             for n in range(pieces)]
    for copy in loads:
        copy.start()
    first = tuple(across[0] * (1 - q) + across[1] * q for q in parity)
    second = tuple(across[1] * (1 - q) + across[0] * q for q in parity)

    def source(d):
        bits = [1 << n for n in range(n_grp.bit_length()) if d & (1 << n)]
        return grp + sum(bit * (1 - 2 * ((grp // bit) % 2)) for bit in bits)

    barrier = pltpu.get_barrier_semaphore()
    for d in range(1, n_grp):
        for q in parity:
            pl.semaphore_signal(barrier, inc=1, device_id=(chip * 2 + q, source(d)), device_id_type=MESH)
    pl.semaphore_signal(barrier, inc=1, device_id=(mate, grp), device_id_type=MESH)
    for to in across:
        for q in parity:
            pl.semaphore_signal(barrier, inc=1, device_id=(to * 2 + q, grp), device_id_type=MESH)

    def coded(fraction):
        return jnp.round(fraction * 65535.0) - 32768.0

    def decoded(code):
        return (code.astype(jnp.float32) + 32768.0) * (1.0 / 65535.0)

    for copy in small:
        copy.wait()
    meta_ref[...] = jnp.zeros_like(meta_ref)
    meta_ref[0:1, 0:rows] = band_ref[...].astype(jnp.float32)
    meta_ref[1:2, 0:rows] = (tile_ref[...] * TL + first_ref[...]).astype(jnp.float32)
    meta_ref[2:3, 0:rows] = shift_ref[...].astype(jnp.float32)
    meta_ref[3:4, 0:rows] = coded(part_ref[...])
    fs[0:rows] = coded(frac_ref[...]).astype(jnp.int32).astype(jnp.int16)
    fs[rows:rows + 8] = meta_ref[...].astype(jnp.int32).astype(jnp.int16)

    levels = xn.shape[0] // (rows * fields)
    stride = xf.shape[1] // rows
    for n in range(pieces):
        loads[n].wait()
        for r in range(n * rows // pieces, (n + 1) * rows // pieces):
            for f in range(fields):
                xf[f, r * stride:r * stride + levels] = xn[pl.ds((r * fields + f) * levels, levels)].astype(jnp.float32)
    for l in range(levels):
        for f in range(fields):
            x_ref[l * fields + f] = xf[f, pl.ds(l, rows, stride=stride)].astype(jnp.bfloat16)

    pl.semaphore_wait(barrier, 2 * (n_grp - 1) + 1 + 4)

    def remote(src, dst, send, recv, to):
        return pltpu.make_async_remote_copy(
            src_ref=src, dst_ref=dst, send_sem=send, recv_sem=recv, device_id=to, device_id_type=MESH
        )

    def f_copy(d, g):
        return remote(fs, fr.at[g], f_send.at[d], f_recv.at[g], (lat, source(d)))

    def n_copy(d):
        g = source(d)
        src = fs if d == 0 else fr.at[g]
        return remote(src, fr.at[n_grp + g], n_send.at[d], n_recv.at[g], (mate, grp))

    def z_copy(d, v, j, g):
        to, q = source(d), parity[j]
        return remote(x_ref.at[(to * 2 + q) * units + v], xs.at[j * n_grp + g, v],
                      z_send.at[d, j, v], z_recv.at[g, j, v], (chip * 2 + q, to))

    def x_copy():
        return remote(x_ref.at[pl.ds((grp * 2 + other) * units, units)], xs.at[n_grp + grp],
                      x_send, x_recv, (mate, grp))

    def d_copy(v, j):
        return remote(s1.at[v, j, 0], q1.at[v, j], d_send.at[v, j], d_recv.at[v, j], (first[j] * 2 + parity[j], grp))

    def p_copy(v, j):
        return remote(s1.at[v, j, 1], r1.at[v, j], p_send.at[v, j], p_recv.at[v, j], (first[j] * 2 + core, grp))

    def e_copy(v, j):
        return remote(s2.at[v, j], q2.at[v, j], e_send.at[v, j], e_recv.at[v, j], (second[j] * 2 + parity[j], grp))

    def o_copy(v):
        return remote(s3.at[v], r3.at[v], o_send.at[v], o_recv.at[v], (mate, grp))

    own_x = pltpu.make_async_copy(x_ref.at[pl.ds((grp * 2 + core) * units, units)], xs.at[grp], loc_sem)
    for d in range(1, n_grp):
        f_copy(n_grp - d, grp).start()
    n_copy(0).start()
    def issue(v):
        for d in range(n_grp - 1, 0, -1):
            for j in range(2):
                z_copy(d, v, j, grp).start()

    for v in range(units):
        for near in range(2 * v, min(2 * v + 2, units)):
            for j in range(2):
                z_copy(1, near, j, grp).start()
        for d in range(2, n_grp):
            for j in range(2):
                z_copy(d, v, j, grp).start()
    own_x.start()
    x_copy().start()

    lane = lax.broadcasted_iota(jnp.int32, (rows, points), 1)
    eye = lax.broadcasted_iota(jnp.int32, (rows, points), 0) == lane
    steps = (1, 2, 4, 8, 16)

    def turn(values, amount):
        return pltpu.roll(values, amount % points, 1)

    def weights_of(at, code):
        shift_lanes = code[rows:rows + 8].astype(jnp.int32)[2:3].astype(jnp.float32)
        diagonal = jnp.where(eye, shift_lanes, 0.0).astype(jnp.bfloat16)
        shift = jnp.dot(
            diagonal, jnp.ones((points, points), jnp.bfloat16), preferred_element_type=jnp.float32
        ).astype(jnp.int32)
        bits = shift + 8
        for m, weight in enumerate(lagrange(decoded(code[0:rows].astype(jnp.int32)))):
            weight = weight.astype(jnp.bfloat16).astype(jnp.float32)
            for step in steps:
                weight = jnp.where((bits & step) != 0, turn(weight, step), weight)
            weight = turn(weight, m - 9)
            raw = lane - shift - (m - 1)
            inside = (raw >= 0) & (raw < points)
            wl[at, m] = jnp.where(inside, weight, 0.0)
            wl[at, 4 + m] = jnp.where(inside, 0.0, weight)
        wl[at, 8] = bits.astype(jnp.float32)

    wide = lax.broadcasted_iota(jnp.int32, (8, 2 * rows), 1)
    slot = lax.broadcasted_iota(jnp.int32, (tile_rows, 2 * rows), 0)

    def meta_of(at):
        return fr[at, rows:rows + 8].astype(jnp.int32).astype(jnp.float32)

    def table_of(at):
        both = jnp.where(wide < rows, meta_of(at), pltpu.roll(meta_of(at + 1), rows, 1))
        band = both[0:1].astype(jnp.int32)
        place = both[1:2].astype(jnp.int32)
        lat_weight = [w.astype(jnp.bfloat16).astype(jnp.float32) for w in lagrange(decoded(both[3:4]))]
        for j in range(2):
            for e, to in enumerate((chip, first[j], second[j], opposite)):
                far = slot - jnp.where(band == to * 2 + parity[j], place, -(1 << 20))
                table = jnp.zeros(far.shape, jnp.float32)
                for k in range(4):
                    table = jnp.where(far == k, lat_weight[k], table)
                am[pl.ds(BLOCKS.index((j, e)) * tile_rows, tile_rows), pl.ds(at * rows, 2 * rows)] = table.astype(jnp.bfloat16)

    fr[grp] = fs[...]
    weights_of(grp, fs[...])
    for d in range(1, n_grp):
        f_copy(d, source(d)).wait_recv()
        n_copy(d).start()
        weights_of(source(d), fr[source(d)])
    for g in range(0, n_grp, 2):
        table_of(g)
    for d in range(n_grp):
        g = source(d)
        n_copy(d).wait_recv()
        weights_of(n_grp + g, fr[n_grp + g])
    for g in range(0, n_grp, 2):
        table_of(n_grp + g)
    own_x.wait()
    x_copy().wait_recv()

    def lon(at, v):
        bits = wl[at, 8].astype(jnp.int32)
        moved = xs[at, v].astype(jnp.float32)
        for step in steps:
            moved = jnp.where((bits & step) != 0, turn(moved, step), moved)
        own, spill = 0.0, 0.0
        for m in range(4):
            x = turn(moved, m - 9)
            own = own + x * wl[at, m]
            spill = spill + x * wl[at, 4 + m]
        place = pl.ds(at * rows, rows)
        rb[v % 2, place, 0:points] = own.astype(jnp.bfloat16)
        rb[v % 2, place, points:2 * points] = spill.astype(jnp.bfloat16)

    low = lax.broadcasted_iota(jnp.int32, (tile_rows, points), 1) < points // 2

    def arrive(v):
        for d in range(n_grp):
            for j in range(2):
                if d:
                    z_copy(d, v, j, source(d)).wait_recv()
            for j in range(2):
                lon(j * n_grp + source(d), v)

    def depart(v):
        for part in range(1):
            count = len(BLOCKS) * tile_rows
            whole = jnp.dot(am[pl.ds(part * count, count)], rb[v % 2], preferred_element_type=jnp.float32)
            for at, (j, e) in enumerate(BLOCKS):
                both = whole[at * tile_rows:(at + 1) * tile_rows]
                own, spill = both[:, :points], both[:, points:]
                ahead = jnp.concatenate([spill[-TL:], spill[:-TL]], axis=0)
                behind = jnp.concatenate([spill[TL:], spill[:TL]], axis=0)
                total = own + jnp.where(low, ahead, behind)
                if e == 3:
                    s1[v, j, 1] = total.astype(jnp.bfloat16)
                    p_copy(v, j).start()
                elif e == 1:
                    s1[v, j, 0] = total.astype(jnp.bfloat16)
                    d_copy(v, j).start()
                elif e == 2:
                    pb[v % 2, j] = total
                elif j == 0:
                    out_ref[core * units + v] = total
                else:
                    s3[v] = total
                    o_copy(v).start()

    def middle(v):
        for j in range(2):
            p_copy(v, j).wait_recv()
            s2[v, j] = (pb[v % 2, j] + r1[v, j].astype(jnp.float32)).astype(jnp.bfloat16)
            e_copy(v, j).start()

    def finish(v):
        for j in range(2):
            d_copy(v, j).wait_recv()
            e_copy(v, j).wait_recv()
            at = parity[j] * units + v
            if j:
                o_copy(v).wait_recv()
            mine = r3[v] if j else out_ref[at]
            out_ref[at] = mine + q1[v, j].astype(jnp.float32) + q2[v, j].astype(jnp.float32)

    def chunk(v, carry):
        @pl.when(v < units)
        def _():
            arrive(v)

            depart(v)

        @pl.when((v >= 1) & (v < units + 1))
        def _():
            middle(v - 1)

        @pl.when(v >= 2)
        def _():
            finish(v - 2)

        return carry

    lax.fori_loop(0, units + 2, chunk, 0)

    n_copy(0).wait_send()
    x_copy().wait_send()
    for d in range(1, n_grp):
        f_copy(d, grp).wait_send()
        n_copy(d).wait_send()
    for v in range(units):
        o_copy(v).wait_send()
        for j in range(2):
            for d in range(1, n_grp):
                z_copy(d, v, j, grp).wait_send()
            d_copy(v, j).wait_send()
            p_copy(v, j).wait_send()
            e_copy(v, j).wait_send()


def fused(increments, band, tile_index, lat_offset, lon_shift, lat_frac, lon_frac):
    rows, fields, all_levels, points = increments.shape
    n_lat, n_grp = lax.axis_size("lat"), lax.axis_size("grp")
    n_chip = n_lat // 2
    levels = all_levels // n_grp
    tile_rows = TILES_DEV * TL
    units = levels * fields // 2
    x = increments.reshape(rows * fields * all_levels, points)
    small = [a.reshape(1, rows) for a in (band, tile_index, lat_offset, lon_shift, lat_frac)]
    bf16, f32 = jnp.bfloat16, jnp.float32
    dma = pltpu.SemaphoreType.DMA
    sums = (units, 2, tile_rows, points)
    return pl.pallas_call(
        functools.partial(fused_kernel, n_lat, n_grp, fields),
        out_shape=jax.ShapeDtypeStruct((2 * units, tile_rows, points), f32),
        in_specs=[pl.BlockSpec(memory_space=pltpu.HBM)] * 7,
        out_specs=pl.BlockSpec(memory_space=pltpu.VMEM),
        scratch_shapes=[
            pltpu.VMEM((rows, points), f32),
            *[pltpu.VMEM((1, rows), a.dtype) for a in small],
            pltpu.VMEM((rows * fields * all_levels, points), bf16),
            pltpu.VMEM((fields, rows * (all_levels + 8), points), f32),
            pltpu.VMEM((all_levels * fields, rows, points), bf16),
            pltpu.VMEM((8, points), f32),
            pltpu.VMEM((rows + 8, points), jnp.int16),
            pltpu.VMEM((2 * n_grp, units, rows, points), bf16),
            pltpu.VMEM((2 * n_grp, rows + 8, points), jnp.int16),
            pltpu.VMEM((2 * n_grp, 9, rows, points), f32),
            pltpu.VMEM((n_lat * tile_rows, n_grp * 2 * rows), bf16),
            pltpu.VMEM((2, n_grp * 2 * rows, 2 * points), bf16),
            pltpu.VMEM((2, 2, tile_rows, points), f32),
            pltpu.VMEM((units, 2, 2, tile_rows, points), bf16),
            pltpu.VMEM(sums, bf16),
            pltpu.VMEM(sums, bf16),
            pltpu.VMEM(sums, bf16),
            pltpu.VMEM(sums, bf16),
            pltpu.VMEM((units, tile_rows, points), f32),
            pltpu.VMEM((units, tile_rows, points), f32),
            dma((n_grp, 2, units)),
            dma((n_grp, 2, units)),
            dma((n_grp,)),
            dma((n_grp,)),
            dma((n_grp,)),
            dma((n_grp,)),
            dma,
            dma,
            dma((units, 2)),
            dma((units, 2)),
            dma((units, 2)),
            dma((units, 2)),
            dma((units, 2)),
            dma((units, 2)),
            dma((units,)),
            dma((units,)),
            dma,
            dma((4,)),
            dma((6,)),
        ],
        compiler_params=pltpu.CompilerParams(
            collective_id=0, has_side_effects=True, vmem_limit_bytes=54525952
        ),
    )(x, lon_frac, *small).reshape(levels, fields, tile_rows, points)


def solution(mesh):
    in_specs = (
        P(("lat", "grp"), None, None, None),
        P(("lat", "grp"), None),
        P(("lat", "grp")),
        P(("lat", "grp")),
        P(("lat", "grp")),
        P(("lat", "grp")),
        P(("lat", "grp"), None),
    )
    out_specs = P("grp", None, "lat", None)
    n_lat, n_grp = mesh.shape["lat"], mesh.shape["grp"]

    def local(increments, *rest):
        rows = increments.shape[0]
        dense_rows = n_lat // 2 * TILES_DEV * TL
        slot_rows = n_grp * n_lat * (3 * rows // n_lat)
        grid = n_lat == 8 and n_grp > 1 and n_grp & (n_grp - 1) == 0
        step = fused if grid and dense_rows <= slot_rows else by_slots
        return step(increments, *rest)

    return jax.shard_map(local, mesh=mesh, in_specs=in_specs, out_specs=out_specs, check_vma=False)
```

```python
import functools
import math

import jax
import jax.numpy as jnp
from jax import lax
from jax.experimental import pallas as pl
from jax.experimental.pallas import tpu as pltpu
from jax.sharding import PartitionSpec as P

TL = 16
TILES_DEV = 8


def lagrange(fraction):
    return [
        -fraction * (fraction - 1.0) * (fraction - 2.0) / 6.0,
        (fraction + 1.0) * (fraction - 1.0) * (fraction - 2.0) / 2.0,
        -(fraction + 1.0) * fraction * (fraction - 2.0) / 2.0,
        (fraction + 1.0) * fraction * (fraction - 1.0) / 6.0,
    ]


def lon_adjoint(increments, lon_shift, lon_frac):
    row_count, fields, levels, points = increments.shape
    lon_weight = [w.astype(jnp.bfloat16) for w in lagrange(lon_frac)]
    source = jnp.arange(points, dtype=jnp.int32)[None, :, None]
    target = jnp.arange(points, dtype=jnp.int32)[None, None, :]
    width = math.gcd(row_count, 32)
    nothing = jnp.zeros((), jnp.bfloat16)

    def one_block(number):
        first = number * width
        shifts = lax.dynamic_slice_in_dim(lon_shift, first, width, 0)
        own_matrix = jnp.zeros((width, points, points), jnp.bfloat16)
        spill_matrix = jnp.zeros((width, points, points), jnp.bfloat16)
        for m in range(4):
            weight = lax.dynamic_slice_in_dim(lon_weight[m], first, width, 0)[:, :, None]
            landing = source + shifts[:, None, None] + m - 1
            own_matrix = own_matrix + jnp.where(target == landing, weight, nothing)
            wrapped = (target == landing - points) | (target == landing + points)
            spill_matrix = spill_matrix + jnp.where(wrapped, weight, nothing)
        values = lax.dynamic_slice_in_dim(increments, first, width, 0)
        own = jnp.einsum(
            "bflj,bjc->bflc", values, own_matrix, preferred_element_type=jnp.float32
        ).astype(jnp.bfloat16)
        spill = jnp.einsum(
            "bflj,bjc->bflc", values, spill_matrix, preferred_element_type=jnp.float32
        ).astype(jnp.bfloat16)
        return (own, spill)

    own, spill = lax.map(one_block, jnp.arange(row_count // width, dtype=jnp.int32))
    return (
        own.reshape(row_count, fields, levels, points),
        spill.reshape(row_count, fields, levels, points),
    )


def tile_terms(columns, own_rows, spill_rows):
    points = own_rows.shape[3]
    low_half = (jnp.arange(points, dtype=jnp.int32) < points // 2)[None, None, None, :]
    nothing = jnp.zeros((), jnp.bfloat16)
    spill_next = jnp.where(low_half, spill_rows, nothing)
    spill_prev = jnp.where(low_half, nothing, spill_rows)
    result = jnp.einsum("sq,sflc->lfqc", columns[0], own_rows, preferred_element_type=jnp.float32)
    result = result + jnp.einsum(
        "sq,sflc->lfqc", columns[1], spill_next, preferred_element_type=jnp.float32
    )
    return result + jnp.einsum(
        "sq,sflc->lfqc", columns[2], spill_prev, preferred_element_type=jnp.float32
    )


def by_slots(increments, band, tile_index, lat_offset, lon_shift, lat_frac, lon_frac):
    row_count, fields, levels, points = increments.shape
    n_lat = lax.axis_size("lat")
    capacity = 3 * row_count // n_lat
    tile_rows = TILES_DEV * TL
    own, spill = lon_adjoint(increments, lon_shift, lon_frac)
    lat_weight = [w.astype(jnp.bfloat16) for w in lagrange(lat_frac)]
    tile_slots = jnp.arange(tile_rows, dtype=jnp.int32)[None, :]
    nothing = jnp.zeros((), jnp.bfloat16)

    def stencil_columns(tile_number):
        base_row = tile_number * TL + lat_offset
        table = jnp.zeros((row_count, tile_rows), jnp.bfloat16)
        for k in range(4):
            table = table + jnp.where(
                tile_slots == base_row[:, None] + k, lat_weight[k][:, None], nothing
            )
        return table

    here_columns = stencil_columns(tile_index)
    next_columns = stencil_columns((tile_index + 1) % TILES_DEV)
    prev_columns = stencil_columns((tile_index + TILES_DEV - 1) % TILES_DEV)
    destination = band[:, 0]
    one_hot = (destination[:, None] == jnp.arange(n_lat, dtype=jnp.int32)[None, :]).astype(
        jnp.int32
    )
    position = jnp.sum(jnp.cumsum(one_hot, axis=0) * one_hot, axis=1) - 1
    slot_index = destination * capacity + position

    def to_slots(values):
        empty = jnp.zeros((n_lat * capacity,) + values.shape[1:], jnp.bfloat16)
        placed = empty.at[slot_index].set(values)
        return placed.reshape((n_lat, capacity) + values.shape[1:])

    send_own = to_slots(own)
    send_spill = to_slots(spill)
    send_here = to_slots(here_columns)
    send_next = to_slots(next_columns)
    send_prev = to_slots(prev_columns)
    got = (
        lax.all_to_all(send_own, "lat", split_axis=0, concat_axis=0, tiled=True),
        lax.all_to_all(send_spill, "lat", split_axis=0, concat_axis=0, tiled=True),
        lax.all_to_all(send_here, "lat", split_axis=0, concat_axis=0, tiled=True),
        lax.all_to_all(send_next, "lat", split_axis=0, concat_axis=0, tiled=True),
        lax.all_to_all(send_prev, "lat", split_axis=0, concat_axis=0, tiled=True),
    )
    flat_own = got[0].reshape(-1, fields, levels, points)
    flat_spill = got[1].reshape(-1, fields, levels, points)
    flat_columns = (
        got[2].reshape(-1, tile_rows),
        got[3].reshape(-1, tile_rows),
        got[4].reshape(-1, tile_rows),
    )
    return lax.psum_scatter(
        tile_terms(flat_columns, flat_own, flat_spill), "grp", scatter_dimension=0, tiled=True
    )


MESH = pl.DeviceIdType.MESH
BLOCKS = ((0, 3), (1, 3), (0, 1), (1, 1), (1, 0), (0, 2), (1, 2), (0, 0))
WINDOW = 2


def fused_kernel(n_lat, n_grp, fields, x_hbm, frac_hbm, band_hbm, tile_hbm, first_hbm, shift_hbm, part_hbm, out_ref,
                 frac_ref, band_ref, tile_ref, first_ref, shift_ref, part_ref, xn, xf, x_ref, meta_ref, fs, xs, fr, wl, am, rb, pb, s1, r1, q1, s2, q2, s3, r3,
                 z_send, z_recv, f_send, f_recv, n_send, n_recv, x_send, x_recv,
                 d_send, d_recv, p_send, p_recv, e_send, e_recv, o_send, o_recv, loc_sem, in_sem, small_sem):
    lat = lax.axis_index("lat")
    grp = lax.axis_index("grp")
    chip, core = lat // 2, lat % 2
    other = 1 - core
    mate = chip * 2 + other
    n_chip = n_lat // 2
    units, rows, points = xs.shape[1:]
    tile_rows = TILES_DEV * TL

    def toggled(bit):
        return chip + bit * (1 - 2 * ((chip // bit) % 2))

    across = (toggled(1), toggled(2))
    opposite = toggled(1) + toggled(2) - chip
    parity = (core, other)
    small = [pltpu.make_async_copy(src, dst, small_sem.at[n]) for n, (src, dst) in enumerate(
        ((frac_hbm, frac_ref), (band_hbm, band_ref), (tile_hbm, tile_ref), (first_hbm, first_ref),
         (shift_hbm, shift_ref), (part_hbm, part_ref)))]
    for copy in small:
        copy.start()
    pieces = in_sem.shape[0]
    stretch = xn.shape[0] // pieces
    loads = [pltpu.make_async_copy(x_hbm.at[pl.ds(n * stretch, stretch)], xn.at[pl.ds(n * stretch, stretch)], in_sem.at[n])
             for n in range(pieces)]
    for copy in loads:
        copy.start()
    first = tuple(across[0] * (1 - q) + across[1] * q for q in parity)
    second = tuple(across[1] * (1 - q) + across[0] * q for q in parity)

    def source(d):
        bits = [1 << n for n in range(n_grp.bit_length()) if d & (1 << n)]
        return grp + sum(bit * (1 - 2 * ((grp // bit) % 2)) for bit in bits)

    barrier = pltpu.get_barrier_semaphore()
    for d in range(1, n_grp):
        for q in parity:
            pl.semaphore_signal(barrier, inc=1, device_id=(chip * 2 + q, source(d)), device_id_type=MESH)
    pl.semaphore_signal(barrier, inc=1, device_id=(mate, grp), device_id_type=MESH)
    for to in across:
        for q in parity:
            pl.semaphore_signal(barrier, inc=1, device_id=(to * 2 + q, grp), device_id_type=MESH)

    def coded(fraction):
        return jnp.round(fraction * 65535.0) - 32768.0

    def decoded(code):
        return (code.astype(jnp.float32) + 32768.0) * (1.0 / 65535.0)

    for copy in small:
        copy.wait()
    meta_ref[...] = jnp.zeros_like(meta_ref)
    meta_ref[0:1, 0:rows] = band_ref[...].astype(jnp.float32)
    meta_ref[1:2, 0:rows] = (tile_ref[...] * TL + first_ref[...]).astype(jnp.float32)
    meta_ref[2:3, 0:rows] = shift_ref[...].astype(jnp.float32)
    meta_ref[3:4, 0:rows] = coded(part_ref[...])
    fs[0:rows] = coded(frac_ref[...]).astype(jnp.int32).astype(jnp.int16)
    fs[rows:rows + 8] = meta_ref[...].astype(jnp.int32).astype(jnp.int16)

    levels = xn.shape[0] // (rows * fields)
    stride = xf.shape[1] // rows
    for n in range(pieces):
        loads[n].wait()
        for r in range(n * rows // pieces, (n + 1) * rows // pieces):
            for f in range(fields):
                xf[f, r * stride:r * stride + levels] = xn[pl.ds((r * fields + f) * levels, levels)].astype(jnp.float32)
    for l in range(levels):
        for f in range(fields):
            x_ref[l * fields + f] = xf[f, pl.ds(l, rows, stride=stride)].astype(jnp.bfloat16)

    pl.semaphore_wait(barrier, 2 * (n_grp - 1) + 1 + 4)

    def remote(src, dst, send, recv, to):
        return pltpu.make_async_remote_copy(
            src_ref=src, dst_ref=dst, send_sem=send, recv_sem=recv, device_id=to, device_id_type=MESH
        )

    def f_copy(d, g):
        return remote(fs, fr.at[g], f_send.at[d], f_recv.at[g], (lat, source(d)))

    def n_copy(d):
        g = source(d)
        src = fs if d == 0 else fr.at[g]
        return remote(src, fr.at[n_grp + g], n_send.at[d], n_recv.at[g], (mate, grp))

    def z_copy(d, v, j, g):
        to, q = source(d), parity[j]
        return remote(x_ref.at[(to * 2 + q) * units + v], xs.at[j * n_grp + g, v],
                      z_send.at[d, j, v], z_recv.at[g, j, v], (chip * 2 + q, to))

    def x_copy():
        return remote(x_ref.at[pl.ds((grp * 2 + other) * units, units)], xs.at[n_grp + grp],
                      x_send, x_recv, (mate, grp))

    def d_copy(v, j):
        return remote(s1.at[v, j, 0], q1.at[v, j], d_send.at[v, j], d_recv.at[v, j], (first[j] * 2 + parity[j], grp))

    def p_copy(v, j):
        return remote(s1.at[v, j, 1], r1.at[v, j], p_send.at[v, j], p_recv.at[v, j], (first[j] * 2 + core, grp))

    def e_copy(v, j):
        return remote(s2.at[v, j], q2.at[v, j], e_send.at[v, j], e_recv.at[v, j], (second[j] * 2 + parity[j], grp))

    def o_copy(v):
        return remote(s3.at[v], r3.at[v], o_send.at[v], o_recv.at[v], (mate, grp))

    own_x = pltpu.make_async_copy(x_ref.at[pl.ds((grp * 2 + core) * units, units)], xs.at[grp], loc_sem)
    for d in range(1, n_grp):
        f_copy(n_grp - d, grp).start()
    n_copy(0).start()
    def issue(v):
        for d in range(1, n_grp):
            for j in range(2):
                z_copy(d, v, j, grp).start()

    for v in range(4):
        issue(v)
    own_x.start()
    x_copy().start()

    lane = lax.broadcasted_iota(jnp.int32, (rows, points), 1)
    eye = lax.broadcasted_iota(jnp.int32, (rows, points), 0) == lane
    steps = (1, 2, 4, 8, 16)

    def turn(values, amount):
        return pltpu.roll(values, amount % points, 1)

    def weights_of(at, code):
        shift_lanes = code[rows:rows + 8].astype(jnp.int32)[2:3].astype(jnp.float32)
        diagonal = jnp.where(eye, shift_lanes, 0.0).astype(jnp.bfloat16)
        shift = jnp.dot(
            diagonal, jnp.ones((points, points), jnp.bfloat16), preferred_element_type=jnp.float32
        ).astype(jnp.int32)
        bits = shift + 8
        for m, weight in enumerate(lagrange(decoded(code[0:rows].astype(jnp.int32)))):
            weight = weight.astype(jnp.bfloat16).astype(jnp.float32)
            for step in steps:
                weight = jnp.where((bits & step) != 0, turn(weight, step), weight)
            weight = turn(weight, m - 9)
            raw = lane - shift - (m - 1)
            inside = (raw >= 0) & (raw < points)
            wl[at, m] = jnp.where(inside, weight, 0.0)
            wl[at, 4 + m] = jnp.where(inside, 0.0, weight)
        wl[at, 8] = bits.astype(jnp.float32)

    wide = lax.broadcasted_iota(jnp.int32, (8, 2 * rows), 1)
    slot = lax.broadcasted_iota(jnp.int32, (tile_rows, 2 * rows), 0)

    def meta_of(at):
        return fr[at, rows:rows + 8].astype(jnp.int32).astype(jnp.float32)

    def table_of(at):
        both = jnp.where(wide < rows, meta_of(at), pltpu.roll(meta_of(at + 1), rows, 1))
        band = both[0:1].astype(jnp.int32)
        place = both[1:2].astype(jnp.int32)
        lat_weight = [w.astype(jnp.bfloat16).astype(jnp.float32) for w in lagrange(decoded(both[3:4]))]
        for j in range(2):
            for e, to in enumerate((chip, first[j], second[j], opposite)):
                far = slot - jnp.where(band == to * 2 + parity[j], place, -(1 << 20))
                table = jnp.zeros(far.shape, jnp.float32)
                for k in range(4):
                    table = jnp.where(far == k, lat_weight[k], table)
                am[pl.ds(BLOCKS.index((j, e)) * tile_rows, tile_rows), pl.ds(at * rows, 2 * rows)] = table.astype(jnp.bfloat16)

    fr[grp] = fs[...]
    weights_of(grp, fs[...])
    for d in range(1, n_grp):
        f_copy(d, source(d)).wait_recv()
        n_copy(d).start()
        weights_of(source(d), fr[source(d)])
    for g in range(0, n_grp, 2):
        table_of(g)
    for d in range(n_grp):
        g = source(d)
        n_copy(d).wait_recv()
        weights_of(n_grp + g, fr[n_grp + g])
    for g in range(0, n_grp, 2):
        table_of(n_grp + g)
    own_x.wait()
    x_copy().wait_recv()

    def lon(at, v):
        bits = wl[at, 8].astype(jnp.int32)
        moved = xs[at, v].astype(jnp.float32)
        for step in steps:
            moved = jnp.where((bits & step) != 0, turn(moved, step), moved)
        own, spill = 0.0, 0.0
        for m in range(4):
            x = turn(moved, m - 9)
            own = own + x * wl[at, m]
            spill = spill + x * wl[at, 4 + m]
        place = pl.ds(at * rows, rows)
        rb[v % 2, place, 0:points] = own.astype(jnp.bfloat16)
        rb[v % 2, place, points:2 * points] = spill.astype(jnp.bfloat16)

    low = lax.broadcasted_iota(jnp.int32, (tile_rows, points), 1) < points // 2

    def arrive(v):
        for d in range(n_grp):
            for j in range(2):
                if d:
                    z_copy(d, v, j, source(d)).wait_recv()
            for j in range(2):
                lon(j * n_grp + source(d), v)

    def depart(v):
        for part in range(1):
            count = len(BLOCKS) * tile_rows
            whole = jnp.dot(am[pl.ds(part * count, count)], rb[v % 2], preferred_element_type=jnp.float32)
            for at, (j, e) in enumerate(BLOCKS):
                both = whole[at * tile_rows:(at + 1) * tile_rows]
                own, spill = both[:, :points], both[:, points:]
                ahead = jnp.concatenate([spill[-TL:], spill[:-TL]], axis=0)
                behind = jnp.concatenate([spill[TL:], spill[:TL]], axis=0)
                total = own + jnp.where(low, ahead, behind)
                if e == 3:
                    s1[v, j, 1] = total.astype(jnp.bfloat16)
                    p_copy(v, j).start()
                elif e == 1:
                    s1[v, j, 0] = total.astype(jnp.bfloat16)
                    d_copy(v, j).start()
                elif e == 2:
                    pb[v % 4, j] = total
                elif j == 0:
                    out_ref[core * units + v] = total
                else:
                    s3[v] = total
                    o_copy(v).start()

    def middle(v):
        for j in range(2):
            p_copy(v, j).wait_recv()
            s2[v, j] = (pb[v % 4, j] + r1[v, j].astype(jnp.float32)).astype(jnp.bfloat16)
            e_copy(v, j).start()

    def finish(v):
        for j in range(2):
            d_copy(v, j).wait_recv()
            e_copy(v, j).wait_recv()
            at = parity[j] * units + v
            if j:
                o_copy(v).wait_recv()
            mine = r3[v] if j else out_ref[at]
            out_ref[at] = mine + q1[v, j].astype(jnp.float32) + q2[v, j].astype(jnp.float32)

    def chunk(v, carry):
        @pl.when(v < units)
        def _():
            arrive(v)

        @pl.when((v < units - 4))
        def _():
            issue(v + 4)

        @pl.when(v < units)
        def _():
            depart(v)

        @pl.when((v >= 1) & (v < units + 1))
        def _():
            middle(v - 1)

        @pl.when(v >= 3)
        def _():
            finish(v - 3)

        return carry

    lax.fori_loop(0, units + 3, chunk, 0)

    n_copy(0).wait_send()
    x_copy().wait_send()
    for d in range(1, n_grp):
        f_copy(d, grp).wait_send()
        n_copy(d).wait_send()
    for v in range(units):
        o_copy(v).wait_send()
        for j in range(2):
            for d in range(1, n_grp):
                z_copy(d, v, j, grp).wait_send()
            d_copy(v, j).wait_send()
            p_copy(v, j).wait_send()
            e_copy(v, j).wait_send()


def fused(increments, band, tile_index, lat_offset, lon_shift, lat_frac, lon_frac):
    rows, fields, all_levels, points = increments.shape
    n_lat, n_grp = lax.axis_size("lat"), lax.axis_size("grp")
    n_chip = n_lat // 2
    levels = all_levels // n_grp
    tile_rows = TILES_DEV * TL
    units = levels * fields // 2
    x = increments.reshape(rows * fields * all_levels, points)
    small = [a.reshape(1, rows) for a in (band, tile_index, lat_offset, lon_shift, lat_frac)]
    bf16, f32 = jnp.bfloat16, jnp.float32
    dma = pltpu.SemaphoreType.DMA
    sums = (units, 2, tile_rows, points)
    return pl.pallas_call(
        functools.partial(fused_kernel, n_lat, n_grp, fields),
        out_shape=jax.ShapeDtypeStruct((2 * units, tile_rows, points), f32),
        in_specs=[pl.BlockSpec(memory_space=pltpu.HBM)] * 7,
        out_specs=pl.BlockSpec(memory_space=pltpu.VMEM),
        scratch_shapes=[
            pltpu.VMEM((rows, points), f32),
            *[pltpu.VMEM((1, rows), a.dtype) for a in small],
            pltpu.VMEM((rows * fields * all_levels, points), bf16),
            pltpu.VMEM((fields, rows * (all_levels + 8), points), f32),
            pltpu.VMEM((all_levels * fields, rows, points), bf16),
            pltpu.VMEM((8, points), f32),
            pltpu.VMEM((rows + 8, points), jnp.int16),
            pltpu.VMEM((2 * n_grp, units, rows, points), bf16),
            pltpu.VMEM((2 * n_grp, rows + 8, points), jnp.int16),
            pltpu.VMEM((2 * n_grp, 9, rows, points), f32),
            pltpu.VMEM((n_lat * tile_rows, n_grp * 2 * rows), bf16),
            pltpu.VMEM((2, n_grp * 2 * rows, 2 * points), bf16),
            pltpu.VMEM((4, 2, tile_rows, points), f32),
            pltpu.VMEM((units, 2, 2, tile_rows, points), bf16),
            pltpu.VMEM(sums, bf16),
            pltpu.VMEM(sums, bf16),
            pltpu.VMEM(sums, bf16),
            pltpu.VMEM(sums, bf16),
            pltpu.VMEM((units, tile_rows, points), f32),
            pltpu.VMEM((units, tile_rows, points), f32),
            dma((n_grp, 2, units)),
            dma((n_grp, 2, units)),
            dma((n_grp,)),
            dma((n_grp,)),
            dma((n_grp,)),
            dma((n_grp,)),
            dma,
            dma,
            dma((units, 2)),
            dma((units, 2)),
            dma((units, 2)),
            dma((units, 2)),
            dma((units, 2)),
            dma((units, 2)),
            dma((units,)),
            dma((units,)),
            dma,
            dma((4,)),
            dma((6,)),
        ],
        compiler_params=pltpu.CompilerParams(
            collective_id=0, has_side_effects=True, vmem_limit_bytes=54525952
        ),
    )(x, lon_frac, *small).reshape(levels, fields, tile_rows, points)


def solution(mesh):
    in_specs = (
        P(("lat", "grp"), None, None, None),
        P(("lat", "grp"), None),
        P(("lat", "grp")),
        P(("lat", "grp")),
        P(("lat", "grp")),
        P(("lat", "grp")),
        P(("lat", "grp"), None),
    )
    out_specs = P("grp", None, "lat", None)
    n_lat, n_grp = mesh.shape["lat"], mesh.shape["grp"]

    def local(increments, *rest):
        rows = increments.shape[0]
        dense_rows = n_lat // 2 * TILES_DEV * TL
        slot_rows = n_grp * n_lat * (3 * rows // n_lat)
        grid = n_lat == 8 and n_grp > 1 and n_grp & (n_grp - 1) == 0
        step = fused if grid and dense_rows <= slot_rows else by_slots
        return step(increments, *rest)

    return jax.shard_map(local, mesh=mesh, in_specs=in_specs, out_specs=out_specs, check_vma=False)
```
